32 devices in a mesh: blk: 4 (over y, x), inner: 8 (over z, core).
Axes of the slice: x: 2, y: 2, z: 4, core: 2. Of those that a mesh axis runs over, the one named last changes fastest.
Arguments:
- points: float32 [4096, 128], P(('blk', 'inner')), may hold values from -8 to 8
- lengthscales: float32 [128], replicated, may hold values from 6 to 24
- noise_level: float32 [1], replicated, may hold values from 1 to 10
- iterate: float32 [4096, 64], P(('blk', 'inner')), may hold values from -6 to 6
- residual: float32 [4096, 64], P(('blk', 'inner')), may hold values from -6 to 6
- direction: float32 [4096, 64], P(('blk', 'inner')), may hold values from -6 to 6
Outputs:
- new_iterate: float32 [4096, 64], P(('blk', 'inner'))
- new_residual: float32 [4096, 64], P(('blk', 'inner'))
- new_direction: float32 [4096, 64], P(('blk', 'inner'))
The draws below stay inside these ranges and needn't reach their ends.
All inputs are finite; a program needn't handle non-finite values.
Results may differ from the reference program's by a relative error of at most 0.00014.
Values sent between devices are 32-bit elements; how exact they have to be, the bound alone decides.
A program may use at most 64 MiB of HBM per device.

```python
import math
import jax
import jax.numpy as jnp
from jax import lax

D = 128
RHS = 64
PTS_DEV = 128
NPTS = 4096


def draw_points(key, part):
    clusters = max(NPTS // 128, 4)
    key_member = jax.random.fold_in(key, 101)
    key_centre = jax.random.fold_in(key, 202)
    key_spread = jax.random.fold_in(key, 404)
    member = jax.random.randint(key_member, (NPTS,), 0, clusters)
    centres = 2.0 * jax.random.normal(key_centre, (clusters, D), jnp.float32)
    spread = jax.random.normal(key_spread, (NPTS, D), jnp.float32)
    values = centres[member] + spread
    return jnp.clip(values, -8.0, 8.0).astype(jnp.float32)


def block_scale(own_key, shape, pieces, smallest, top_value):
    def one(position, blocks):
        draws = jax.random.uniform(jax.random.fold_in(jax.random.fold_in(own_key, 6), position), (blocks,), jnp.float32, smallest / len(pieces), top_value / len(pieces))
        return jnp.repeat(jnp.exp(draws), shape[position] // blocks).reshape((-1,) + (1,) * (len(shape) - position - 1))

    gain = one(*pieces[0])
    for cut in pieces[1:]:
        gain = gain * one(*cut)
    return gain


def noise(stream_key, extent, scale, limit, pieces=(), dtype=jnp.bfloat16):
    array = jax.random.normal(stream_key, extent, jnp.float32) * scale
    if len(pieces) > 0:
        array = block_scale(stream_key, extent, pieces, -0.22, 0.18) * array
    return jnp.clip(array, min=-limit, max=limit).astype(dtype)


def setup_inputs(seed: int = 0) -> dict:
    seeds = jax.random.split(jax.random.key(seed), 7)
    points = draw_points(jax.random.fold_in(seeds[6], 71), 0)
    lengthscales = jnp.clip(jnp.exp(jax.random.uniform(seeds[1], (D,), jnp.float32, math.log(6.0), math.log(24.0))), 6.0, 24.0)
    noise_level = jnp.clip(jnp.exp(jax.random.uniform(seeds[2], (1,), jnp.float32, math.log(1.0), math.log(10.0))), 1.0, 10.0)
    iterate = noise(seeds[3], (NPTS, RHS), 1.0, 6.0, ((0, 32),), jnp.float32)
    residual = noise(seeds[4], (NPTS, RHS), 1.0, 6.0, ((0, 32),), jnp.float32)
    direction = noise(seeds[5], (NPTS, RHS), 1.0, 6.0, ((0, 32),), jnp.float32)
    return dict(points=points, lengthscales=lengthscales, noise_level=noise_level, iterate=iterate, residual=residual, direction=direction)


def kernel_block(left, left_sq, right, right_sq):
    products = lax.dot_general(left.astype(jnp.float32), right.astype(jnp.float32), (((1,), (1,)), ((), ())), precision=lax.Precision.HIGHEST, preferred_element_type=jnp.float32)
    return jnp.exp(-0.5 * (left_sq[:, None] + right_sq[None, :] - 2.0 * products))

def matmul(left, right):
    return jnp.dot(left.astype(jnp.float32), right.astype(jnp.float32), precision=lax.Precision.HIGHEST, preferred_element_type=jnp.float32)

def transposed(left, right):
    return lax.dot_general(left.astype(jnp.float32), right.astype(jnp.float32), (((0,), (0,)), ((), ())), precision=lax.Precision.HIGHEST, preferred_element_type=jnp.float32)

def chol_solve(matrix, rhs_side):
    factor = jnp.linalg.cholesky(matrix)
    return jax.scipy.linalg.cho_solve((factor, True), rhs_side)

def reference(points, lengthscales, noise_level, iterate, residual, direction):
    scaled = points / lengthscales[None, :]
    sq_norms = jnp.sum(scaled * scaled, axis=1)
    blocks = scaled.reshape(NPTS // PTS_DEV, PTS_DEV, D)
    block_sq = sq_norms.reshape(NPTS // PTS_DEV, PTS_DEV)

    def one_block(pair):
        rows, rows_sq = pair
        return matmul(kernel_block(rows, rows_sq, scaled, sq_norms), direction)
    image = lax.map(one_block, (blocks, block_sq)).reshape(NPTS, RHS)
    image = image + noise_level[0] * direction
    gram_raw = transposed(direction, image)
    gram_matrix = 0.5 * (gram_raw + gram_raw.T)
    res_gram = transposed(residual, residual)
    step_size = chol_solve(gram_matrix, res_gram)
    new_iterate = iterate + matmul(direction, step_size)
    new_residual = residual - matmul(image, step_size)
    new_gram = transposed(new_residual, new_residual)
    correction = chol_solve(res_gram, new_gram)
    new_direction = new_residual + matmul(direction, correction)
    return (new_iterate, new_residual, new_direction)
```

```python
import functools

import jax
import jax.numpy as jnp
from jax import lax
from jax.experimental import pallas as pl
from jax.experimental.pallas import tpu as pltpu
from jax.sharding import PartitionSpec as P

MESH = pl.DeviceIdType.MESH
HI = lax.Precision.HIGHEST


def mm(left, right, dims):
    return lax.dot_general(left, right, (dims, ((), ())), precision=HI, preferred_element_type=jnp.float32)


def nn(left, right):
    return mm(left, right, ((1,), (0,)))


def nt(left, right):
    return mm(left, right, ((1,), (1,)))


def tn(left, right):
    return mm(left, right, ((0,), (0,)))


def pack(value):
    half = value.shape[0] // 2
    return jnp.concatenate([value[:half], value[half:]], axis=1)


def unpack(value):
    half = value.shape[1] // 2
    return jnp.concatenate([value[:, :half], value[:, half:]], axis=0)


def eliminate(matrix, rhs_side):
    n = matrix.shape[0]
    work = jnp.concatenate([matrix, rhs_side], axis=1)
    rows = lax.broadcasted_iota(jnp.int32, work.shape, 0)
    for k in range(n):
        column = jnp.broadcast_to(work[:, k : k + 1], work.shape)
        pivot_row = work[k : k + 1, :] / column[k : k + 1, :]
        work = jnp.where(rows == k, pivot_row, work - column * pivot_row)
    return work[:, n:]


class Exchange:
    def __init__(self, src, slots, send, recv, me, n, device):
        self.src, self.slots, self.send, self.recv = src, slots, send, recv
        self.me, self.n, self.device = me, n, device

    def copy(self, offset, slot):
        return pltpu.make_async_remote_copy(
            src_ref=self.src,
            dst_ref=self.slots.at[slot],
            send_sem=self.send.at[offset],
            recv_sem=self.recv.at[slot],
            device_id=self.device(lax.rem(self.me + offset, self.n)),
            device_id_type=MESH,
        )

    def start(self, value):
        self.src[...] = value
        for offset in range(1, self.n):
            self.copy(offset, self.me).start()

    def finish(self):
        total = self.src[...]
        for offset in range(1, self.n):
            slot = lax.rem(self.me + self.n - offset, self.n)
            self.copy(offset, slot).wait_recv()
            total = total + self.slots[slot]
        for offset in range(1, self.n):
            self.copy(offset, self.me).wait_send()
        return total


def body(sizes, pts, scales, noise, iterate, residual, direction, out_i, out_r, out_d, *scratch):
    nb, nh, rows, rhs = sizes
    cbuf, c_send, c_recv, f_send, rbuf, r_send, r_recv, pout, pin, p_send, p_recv, dall = scratch[:12]
    rest = scratch[12:]
    b = lax.axis_index("blk")
    i = lax.axis_index("inner")
    core = lax.rem(i, 2)
    hi = i // 2
    sibling = {"inner": hi * 2 + 1 - core}

    def at_blk(place):
        return {"blk": place}

    def at_hi(place):
        return {"inner": place * 2 + core}

    def at_core(place):
        return {"inner": hi * 2 + place}

    ways = ((core, 2, at_core), (b, nb, at_blk), (hi, nh, at_hi))
    sums = []
    for which in range(3):
        stages = []
        for stage, (me, n, device) in enumerate(ways):
            src, slots, send, recv = rest[(which * 3 + stage) * 4 : (which * 3 + stage) * 4 + 4]
            stages.append(Exchange(src, slots, send, recv, me, n, device))
        sums.append(stages)
    sum_r, sum_a, sum_bc = sums

    barrier = pltpu.get_barrier_semaphore()
    for offset in range(1, nb):
        pl.semaphore_signal(barrier, inc=1, device_id=at_blk(lax.rem(b + offset, nb)), device_id_type=MESH)
    for offset in range(1, nh):
        pl.semaphore_signal(barrier, inc=1, device_id=at_hi(lax.rem(hi + offset, nh)), device_id_type=MESH)
    pl.semaphore_signal(barrier, inc=1, device_id=sibling, device_id_type=MESH)
    points = pts[...]
    rbuf[hi] = points
    cbuf[core, b, :rows] = points
    cbuf[core, b, rows:] = pack(direction[...])
    res = residual[...]
    own_res_gram = pack(tn(res, res))
    pl.semaphore_wait(barrier, nb + nh - 1)

    def c_copy(offset, slot):
        return pltpu.make_async_remote_copy(
            src_ref=cbuf.at[core, slot],
            dst_ref=cbuf.at[core, slot],
            send_sem=c_send.at[offset],
            recv_sem=c_recv.at[core, slot],
            device_id=at_blk(lax.rem(b + offset, nb)),
            device_id_type=MESH,
        )

    def f_copy(side, slot):
        return pltpu.make_async_remote_copy(
            src_ref=cbuf.at[side, slot],
            dst_ref=cbuf.at[side, slot],
            send_sem=f_send.at[slot],
            recv_sem=c_recv.at[side, slot],
            device_id=sibling,
            device_id_type=MESH,
        )

    def r_copy(offset, slot):
        return pltpu.make_async_remote_copy(
            src_ref=rbuf.at[slot],
            dst_ref=rbuf.at[slot],
            send_sem=r_send.at[offset],
            recv_sem=r_recv.at[slot],
            device_id=at_hi(lax.rem(hi + offset, nh)),
            device_id_type=MESH,
        )

    def p_copy(owner, slot):
        return pltpu.make_async_remote_copy(
            src_ref=pout.at[owner],
            dst_ref=pin.at[slot],
            send_sem=p_send.at[owner],
            recv_sem=p_recv.at[slot],
            device_id=at_hi(owner),
            device_id_type=MESH,
        )

    for offset in range(1, nh):
        r_copy(offset, hi).start()
    for offset in range(1, nb):
        c_copy(offset, b).start()
    f_copy(core, b).start()
    sum_r[0].start(own_res_gram)
    for offset in range(1, nb):
        slot = lax.rem(b + nb - offset, nb)
        c_copy(offset, slot).wait_recv()
        f_copy(core, slot).start()
    sum_r[1].start(sum_r[0].finish())
    for slot in range(nb):
        f_copy(1 - core, slot).wait_recv()

    scale = scales[...]
    for side in range(2):
        for slot in range(nb):
            block = pl.ds((side * nb + slot) * rows, rows)
            dall[block, :] = unpack(cbuf[side, slot, rows:])
    column_pts = jnp.concatenate(
        [cbuf[side, slot, :rows] / scale for side in range(2) for slot in range(nb)], axis=0
    )
    ones = jnp.ones((8, scale.shape[1]), jnp.float32)
    column_sq = 0.5 * nt(ones, column_pts * column_pts)[:1, :]

    def image_rows(place):
        left = rbuf[place] / scale
        left_sq = 0.5 * jnp.sum(left * left, axis=1, keepdims=True)
        tile = jnp.exp(nt(left, column_pts) - (left_sq + column_sq))
        return nn(tile, dall[...])

    image = image_rows(hi)
    for offset in range(1, nh):
        place = lax.rem(hi + nh - offset, nh)
        r_copy(offset, place).wait_recv()
        pout[place] = pack(image_rows(place))
        p_copy(place, hi).start()
    sum_r[2].start(sum_r[1].finish())
    res_gram = unpack(sum_r[2].finish())
    eye = lax.broadcasted_iota(jnp.int32, (rhs, rhs), 0) == lax.broadcasted_iota(jnp.int32, (rhs, rhs), 1)
    res_inverse = eliminate(res_gram, eye.astype(jnp.float32))

    direct = direction[...]
    image = image + noise[0, 0] * direct
    for offset in range(1, nh):
        place = lax.rem(hi + nh - offset, nh)
        p_copy(place, place).wait_recv()
        image = image + unpack(pin[place])
    own_gram = pack(0.5 * (tn(direct, image) + tn(image, direct)))
    sum_a[0].start(own_gram)
    sum_bc[0].start(tn(image, jnp.concatenate([res, image], axis=1)))
    sum_a[1].start(sum_a[0].finish())
    sum_bc[1].start(sum_bc[0].finish())
    sum_a[2].start(sum_a[1].finish())
    sum_bc[2].start(sum_bc[1].finish())
    gram = unpack(sum_a[2].finish())
    step = eliminate(gram, res_gram)
    both = sum_bc[2].finish()
    cross, square = both[:, :rhs], both[:, rhs:]
    moved = nn(square, step) - cross
    new_gram = res_gram + tn(
        jnp.concatenate([step, -cross], axis=0), jnp.concatenate([moved, step], axis=0)
    )
    correction = nn(res_inverse, new_gram)
    new_res = res - nn(image, step)
    out_i[...] = iterate[...] + nn(direct, step)
    out_r[...] = new_res
    out_d[...] = new_res + nn(direct, correction)

    for offset in range(1, nb):
        c_copy(offset, b).wait_send()
    for slot in range(nb):
        f_copy(core, slot).wait_send()
    for offset in range(1, nh):
        r_copy(offset, hi).wait_send()
        place = lax.rem(hi + nh - offset, nh)
        p_copy(place, hi).wait_send()


def solution(mesh):
    nb, ni = mesh.shape["blk"], mesh.shape["inner"]
    nh = ni // 2

    def on_device(points, lengthscales, noise_level, iterate, residual, direction):
        rows, features = points.shape
        rhs = direction.shape[1]
        f32, dma = jnp.float32, pltpu.SemaphoreType.DMA
        half = rows // 2
        scratch = [
            pltpu.VMEM((2, nb, rows + half, features), f32),
            dma((nb,)),
            dma((2, nb)),
            dma((nb,)),
            pltpu.VMEM((nh, rows, features), f32),
            dma((nh,)),
            dma((nh,)),
            pltpu.VMEM((nh, half, 2 * rhs), f32),
            pltpu.VMEM((nh, half, 2 * rhs), f32),
            dma((nh,)),
            dma((nh,)),
            pltpu.VMEM((2 * nb * rows, rhs), f32),
        ]
        for height in (rhs // 2, rhs // 2, rhs):
            for n in (2, nb, nh):
                scratch += [
                    pltpu.VMEM((height, 2 * rhs), f32),
                    pltpu.VMEM((n, height, 2 * rhs), f32),
                    dma((n,)),
                    dma((n,)),
                ]
        vmem = pl.BlockSpec(memory_space=pltpu.VMEM)
        out = jax.ShapeDtypeStruct((rows, rhs), f32)
        return pl.pallas_call(
            functools.partial(body, (nb, nh, rows, rhs)),
            out_shape=(out, out, out),
            in_specs=[vmem, vmem, pl.BlockSpec(memory_space=pltpu.SMEM), vmem, vmem, vmem],
            out_specs=(vmem, vmem, vmem),
            scratch_shapes=scratch,
            compiler_params=pltpu.CompilerParams(collective_id=0, has_side_effects=True),
            name="cg_step",
        )(points, lengthscales[None, :], noise_level[None, :], iterate, residual, direction)

    rows_spec = P(("blk", "inner"), None)
    return jax.shard_map(
        on_device,
        mesh=mesh,
        in_specs=(rows_spec, P(), P(), rows_spec, rows_spec, rows_spec),
        out_specs=(rows_spec, rows_spec, rows_spec),
        check_vma=False,
    )
```

```python
import functools

import jax
import jax.numpy as jnp
from jax import lax
from jax.experimental import pallas as pl
from jax.experimental.pallas import tpu as pltpu
from jax.sharding import PartitionSpec as P

MESH = pl.DeviceIdType.MESH
HI = lax.Precision.HIGHEST


def mm(left, right, dims):
    return lax.dot_general(left, right, (dims, ((), ())), precision=HI, preferred_element_type=jnp.float32)


def nn(left, right):
    return mm(left, right, ((1,), (0,)))


def nt(left, right):
    return mm(left, right, ((1,), (1,)))


def tn(left, right):
    return mm(left, right, ((0,), (0,)))


def pack(value):
    half = value.shape[0] // 2
    return jnp.concatenate([value[:half], value[half:]], axis=1)


def unpack(value):
    half = value.shape[1] // 2
    return jnp.concatenate([value[:, :half], value[:, half:]], axis=0)


def partner(me, offset, n):
    if n & (n - 1):
        return lax.rem(me + offset, n)
    place, bit = me, 1
    while bit < n:
        if offset & bit:
            place = place + bit - 2 * bit * lax.rem(me // bit, 2)
        bit *= 2
    return place


def source(me, offset, n):
    if n & (n - 1):
        return lax.rem(me + n - offset, n)
    return partner(me, offset, n)


def eliminate(matrix, rhs_side):
    n = matrix.shape[0]
    work = jnp.concatenate([matrix, rhs_side], axis=1)
    rows = lax.broadcasted_iota(jnp.int32, work.shape, 0)
    for k in range(0, n, 2):
        column0 = jnp.broadcast_to(work[:, k : k + 1], work.shape)
        column1 = jnp.broadcast_to(work[:, k + 1 : k + 2], work.shape)
        row0, row1 = work[k : k + 1], work[k + 1 : k + 2]
        upper = column1[k : k + 1]
        inverse = 1.0 / column0[k : k + 1]
        lower = column0[k + 1 : k + 2] * inverse
        second = (row1 - lower * row0) / (column1[k + 1 : k + 2] - lower * upper)
        first = (row0 - upper * second) * inverse
        below = work - column0 * first - column1 * second
        work = jnp.where(rows == k, first, jnp.where(rows == k + 1, second, below))
    return work[:, n:]


class Exchange:
    def __init__(self, src, slots, send, recv, me, n, device):
        self.src, self.slots, self.send, self.recv = src, slots, send, recv
        self.me, self.n, self.device = me, n, device

    def copy(self, offset, slot):
        return pltpu.make_async_remote_copy(
            src_ref=self.src,
            dst_ref=self.slots.at[slot],
            send_sem=self.send.at[offset],
            recv_sem=self.recv.at[slot],
            device_id=self.device(partner(self.me, offset, self.n)),
            device_id_type=MESH,
        )

    def start(self, value):
        self.src[...] = value
        for offset in range(1, self.n):
            self.copy(offset, self.me).start()

    def finish(self):
        total = self.src[...]
        for offset in range(1, self.n):
            slot = source(self.me, offset, self.n)
            self.copy(offset, slot).wait_recv()
            total = total + self.slots[slot]
        for offset in range(1, self.n):
            self.copy(offset, self.me).wait_send()
        return total


def body(sizes, pts, scales, noise, iterate, residual, direction, out_i, out_r, out_d, *scratch):
    nb, nh, rows, rhs = sizes
    cbuf, c_send, c_recv, f_send, rbuf, r_send, r_recv = scratch[:7]
    dbuf, d_send, d_recv, pout, pin, p_send, p_recv = scratch[7:14]
    rest = scratch[14:]
    b = lax.axis_index("blk")
    i = lax.axis_index("inner")
    core = lax.rem(i, 2)
    hi = i // 2
    sibling = {"inner": hi * 2 + 1 - core}

    def at_blk(place):
        return {"blk": place}

    def at_hi(place):
        return {"inner": place * 2 + core}

    def at_core(place):
        return {"inner": hi * 2 + place}

    ways = ((core, 2, at_core), (b, nb, at_blk), (hi, nh, at_hi))
    sums = []
    for which in range(3):
        stages = []
        for stage, (me, n, device) in enumerate(ways):
            src, slots, send, recv = rest[(which * 3 + stage) * 4 : (which * 3 + stage) * 4 + 4]
            stages.append(Exchange(src, slots, send, recv, me, n, device))
        sums.append(stages)
    sum_r, sum_a, sum_bc = sums

    barrier = pltpu.get_barrier_semaphore()
    for offset in range(1, nb):
        pl.semaphore_signal(barrier, inc=1, device_id=at_blk(partner(b, offset, nb)), device_id_type=MESH)
    for offset in range(1, nh):
        pl.semaphore_signal(barrier, inc=1, device_id=at_hi(partner(hi, offset, nh)), device_id_type=MESH)
    pl.semaphore_signal(barrier, inc=1, device_id=sibling, device_id_type=MESH)
    cbuf[core, b, :rows] = pts[...]
    cbuf[core, b, rows:] = direction[...]
    res = residual[...]
    direct = direction[...]
    own_res_gram = pack(nt(res, res))
    pl.semaphore_wait(barrier, nb + nh - 1)

    def c_copy(offset, slot):
        return pltpu.make_async_remote_copy(
            src_ref=cbuf.at[core, slot],
            dst_ref=cbuf.at[core, slot],
            send_sem=c_send.at[offset],
            recv_sem=c_recv.at[core, slot],
            device_id=at_blk(partner(b, offset, nb)),
            device_id_type=MESH,
        )

    def f_copy(side, slot):
        return pltpu.make_async_remote_copy(
            src_ref=cbuf.at[side, slot],
            dst_ref=cbuf.at[side, slot],
            send_sem=f_send.at[slot],
            recv_sem=c_recv.at[side, slot],
            device_id=sibling,
            device_id_type=MESH,
        )

    def r_copy(offset, slot):
        return pltpu.make_async_remote_copy(
            src_ref=pts,
            dst_ref=rbuf.at[slot],
            send_sem=r_send.at[offset],
            recv_sem=r_recv.at[slot],
            device_id=at_hi(partner(hi, offset, nh)),
            device_id_type=MESH,
        )

    def d_copy(offset, slot):
        return pltpu.make_async_remote_copy(
            src_ref=direction,
            dst_ref=dbuf.at[slot],
            send_sem=d_send.at[offset],
            recv_sem=d_recv.at[slot],
            device_id=at_hi(partner(hi, offset, nh)),
            device_id_type=MESH,
        )

    def p_copy(owner, slot):
        return pltpu.make_async_remote_copy(
            src_ref=pout.at[owner],
            dst_ref=pin.at[slot],
            send_sem=p_send.at[owner],
            recv_sem=p_recv.at[slot],
            device_id=at_hi(owner),
            device_id_type=MESH,
        )

    for offset in range(1, nb):
        c_copy(offset, b).start()
    for offset in range(1, nh):
        r_copy(offset, hi).start()
    f_copy(core, b).start()
    sum_r[0].start(own_res_gram)
    for offset in range(1, nh):
        d_copy(offset, hi).start()
    sum_r[1].start(sum_r[0].finish())
    for offset in range(1, nb):
        slot = source(b, offset, nb)
        c_copy(offset, slot).wait_recv()
        f_copy(core, slot).start()
    sum_r[2].start(sum_r[1].finish())
    for slot in range(nb):
        f_copy(1 - core, slot).wait_recv()

    scale = scales[...]
    blocks = [(side, slot) for side in range(2) for slot in range(nb)]
    directions = jnp.concatenate([cbuf[side, slot, rows:] for side, slot in blocks], axis=1)
    column_pts = jnp.concatenate([cbuf[side, slot, :rows] / scale for side, slot in blocks], axis=0)
    column_sq = 0.5 * jnp.sum(column_pts * column_pts, axis=1, keepdims=True)
    ones = jnp.ones((8, scale.shape[1]), jnp.float32)

    def image_part(block):
        left = block / scale
        left_sq = 0.5 * nt(ones, left * left)[:1, :]
        tile = jnp.exp(nt(column_pts, left) - (column_sq + left_sq))
        return nn(directions, tile)

    image = image_part(pts[...]) + noise[0, 0] * direct
    parts, others = [image], [direct]
    for offset in range(1, nh):
        place = source(hi, offset, nh)
        r_copy(offset, place).wait_recv()
        part = image_part(rbuf[place])
        pout[place] = part
        p_copy(place, hi).start()
        parts.append(part)
    for offset in range(1, nh):
        place = source(hi, offset, nh)
        d_copy(offset, place).wait_recv()
        others.append(dbuf[place])
    own_gram = 0.5 * nt(jnp.concatenate(others + parts, axis=1), jnp.concatenate(parts + others, axis=1))
    sum_a[0].start(pack(own_gram))
    sum_a[1].start(sum_a[0].finish())

    res_gram = unpack(sum_r[2].finish())
    eye = lax.broadcasted_iota(jnp.int32, (rhs, rhs), 0) == lax.broadcasted_iota(jnp.int32, (rhs, rhs), 1)
    res_inverse = eliminate(res_gram, eye.astype(jnp.float32))

    sum_a[2].start(sum_a[1].finish())
    for offset in range(1, nh):
        place = source(hi, offset, nh)
        p_copy(place, place).wait_recv()
        image = image + pin[place]
    sum_bc[0].start(nt(image, jnp.concatenate([res, image], axis=0)))
    sum_bc[1].start(sum_bc[0].finish())
    sum_bc[2].start(sum_bc[1].finish())
    gram = unpack(sum_a[2].finish())
    step = eliminate(gram, res_gram)
    new_res = res - tn(step, image)
    out_i[...] = iterate[...] + tn(step, direct)
    out_r[...] = new_res
    both = sum_bc[2].finish()
    cross, square = both[:, :rhs], both[:, rhs:]
    moved = nn(square, step) - cross
    new_gram = res_gram + tn(
        jnp.concatenate([step, -cross], axis=0), jnp.concatenate([moved, step], axis=0)
    )
    correction = nn(res_inverse, new_gram)
    out_d[...] = new_res + tn(correction, direct)

    for offset in range(1, nb):
        c_copy(offset, b).wait_send()
    for slot in range(nb):
        f_copy(core, slot).wait_send()
    for offset in range(1, nh):
        r_copy(offset, hi).wait_send()
        d_copy(offset, hi).wait_send()
        p_copy(source(hi, offset, nh), hi).wait_send()


def solution(mesh):
    nb, ni = mesh.shape["blk"], mesh.shape["inner"]
    nh = ni // 2

    def on_device(points, lengthscales, noise_level, iterate, residual, direction):
        rows, features = points.shape
        rhs = direction.shape[1]
        f32, dma = jnp.float32, pltpu.SemaphoreType.DMA
        scratch = [
            pltpu.VMEM((2, nb, rows + rhs, features), f32),
            dma((nb,)),
            dma((2, nb)),
            dma((nb,)),
            pltpu.VMEM((nh, rows, features), f32),
            dma((nh,)),
            dma((nh,)),
            pltpu.VMEM((nh, rhs, rows), f32),
            dma((nh,)),
            dma((nh,)),
            pltpu.VMEM((nh, rhs, rows), f32),
            pltpu.VMEM((nh, rhs, rows), f32),
            dma((nh,)),
            dma((nh,)),
        ]
        for height in (rhs // 2, rhs // 2, rhs):
            for n in (2, nb, nh):
                scratch += [
                    pltpu.VMEM((height, 2 * rhs), f32),
                    pltpu.VMEM((n, height, 2 * rhs), f32),
                    dma((n,)),
                    dma((n,)),
                ]
        vmem = pl.BlockSpec(memory_space=pltpu.VMEM)
        out = jax.ShapeDtypeStruct((rhs, rows), f32)
        results = pl.pallas_call(
            functools.partial(body, (nb, nh, rows, rhs)),
            out_shape=(out, out, out),
            in_specs=[vmem, vmem, pl.BlockSpec(memory_space=pltpu.SMEM), vmem, vmem, vmem],
            out_specs=(vmem, vmem, vmem),
            scratch_shapes=scratch,
            compiler_params=pltpu.CompilerParams(collective_id=0, has_side_effects=True),
            name="cg_step",
        )(points, lengthscales[None, :], noise_level[None, :], iterate.T, residual.T, direction.T)
        return tuple(result.T for result in results)

    rows_spec = P(("blk", "inner"), None)
    return jax.shard_map(
        on_device,
        mesh=mesh,
        in_specs=(rows_spec, P(), P(), rows_spec, rows_spec, rows_spec),
        out_specs=(rows_spec, rows_spec, rows_spec),
        check_vma=False,
    )
```

```python
import functools

import jax
import jax.numpy as jnp
from jax import lax
from jax.experimental import pallas as pl
from jax.experimental.pallas import tpu as pltpu
from jax.sharding import PartitionSpec as P

MESH = pl.DeviceIdType.MESH
HI = lax.Precision.HIGHEST


def mm(left, right, dims):
    return lax.dot_general(left, right, (dims, ((), ())), precision=HI, preferred_element_type=jnp.float32)


def nn(left, right):
    return mm(left, right, ((1,), (0,)))


def nt(left, right):
    return mm(left, right, ((1,), (1,)))


def tn(left, right):
    return mm(left, right, ((0,), (0,)))


def pack(value):
    half = value.shape[0] // 2
    return jnp.concatenate([value[:half], value[half:]], axis=1)


def unpack(value):
    half = value.shape[1] // 2
    return jnp.concatenate([value[:, :half], value[:, half:]], axis=0)


def partner(me, offset, n):
    if n & (n - 1):
        return lax.rem(me + offset, n)
    place, bit = me, 1
    while bit < n:
        if offset & bit:
            place = place + bit - 2 * bit * lax.rem(me // bit, 2)
        bit *= 2
    return place


def source(me, offset, n):
    if n & (n - 1):
        return lax.rem(me + n - offset, n)
    return partner(me, offset, n)


def eliminate(matrix, rhs_side):
    n = matrix.shape[0]
    work = jnp.concatenate([matrix, rhs_side], axis=1)
    rows = lax.broadcasted_iota(jnp.int32, work.shape, 0)
    for k in range(0, n, 2):
        column0 = jnp.broadcast_to(work[:, k : k + 1], work.shape)
        column1 = jnp.broadcast_to(work[:, k + 1 : k + 2], work.shape)
        row0, row1 = work[k : k + 1], work[k + 1 : k + 2]
        upper = column1[k : k + 1]
        inverse = 1.0 / column0[k : k + 1]
        lower = column0[k + 1 : k + 2] * inverse
        second = (row1 - lower * row0) / (column1[k + 1 : k + 2] - lower * upper)
        first = (row0 - upper * second) * inverse
        below = work - column0 * first - column1 * second
        work = jnp.where(rows == k, first, jnp.where(rows == k + 1, second, below))
    return work[:, n:]


class Exchange:
    def __init__(self, src, slots, send, recv, me, n, device):
        self.src, self.slots, self.send, self.recv = src, slots, send, recv
        self.me, self.n, self.device = me, n, device

    def copy(self, offset, slot):
        return pltpu.make_async_remote_copy(
            src_ref=self.src,
            dst_ref=self.slots.at[slot],
            send_sem=self.send.at[offset],
            recv_sem=self.recv.at[slot],
            device_id=self.device(partner(self.me, offset, self.n)),
            device_id_type=MESH,
        )

    def start(self, value):
        self.src[...] = value
        for offset in range(1, self.n):
            self.copy(offset, self.me).start()

    def finish(self):
        total = self.src[...]
        for offset in range(1, self.n):
            slot = source(self.me, offset, self.n)
            self.copy(offset, slot).wait_recv()
            total = total + self.slots[slot]
        for offset in range(1, self.n):
            self.copy(offset, self.me).wait_send()
        return total


def body(sizes, pts, scales, noise, iterate, residual, direction, out, *scratch):
    nb, nh, rows, rhs = sizes
    cbuf, c_send, c_recv, f_send, rbuf, r_send, r_recv = scratch[:7]
    dbuf, d_send, d_recv, pout, pin, p_send, p_recv = scratch[7:14]
    rest = scratch[14:]
    b = lax.axis_index("blk")
    i = lax.axis_index("inner")
    core = lax.rem(i, 2)
    hi = i // 2
    sibling = {"inner": hi * 2 + 1 - core}

    def at_blk(place):
        return {"blk": place}

    def at_hi(place):
        return {"inner": place * 2 + core}

    def at_core(place):
        return {"inner": hi * 2 + place}

    ways = ((core, 2, at_core), (b, nb, at_blk), (hi, nh, at_hi))
    sums = []
    for which in range(3):
        stages = []
        for stage, (me, n, device) in enumerate(ways):
            src, slots, send, recv = rest[(which * 3 + stage) * 4 : (which * 3 + stage) * 4 + 4]
            stages.append(Exchange(src, slots, send, recv, me, n, device))
        sums.append(stages)
    sum_r, sum_a, sum_bc = sums

    barrier = pltpu.get_barrier_semaphore()
    for offset in range(1, nb):
        pl.semaphore_signal(barrier, inc=1, device_id=at_blk(partner(b, offset, nb)), device_id_type=MESH)
    for offset in range(1, nh):
        pl.semaphore_signal(barrier, inc=1, device_id=at_hi(partner(hi, offset, nh)), device_id_type=MESH)
    pl.semaphore_signal(barrier, inc=1, device_id=sibling, device_id_type=MESH)
    cbuf[core, b, :rows] = pts[...]
    cbuf[core, b, rows:] = direction[...]
    res = residual[...]
    direct = direction[...]
    own_res_gram = pack(nt(res, res))
    pl.semaphore_wait(barrier, nb + nh - 1)

    def c_copy(offset, slot):
        return pltpu.make_async_remote_copy(
            src_ref=cbuf.at[core, slot],
            dst_ref=cbuf.at[core, slot],
            send_sem=c_send.at[offset],
            recv_sem=c_recv.at[core, slot],
            device_id=at_blk(partner(b, offset, nb)),
            device_id_type=MESH,
        )

    def f_copy(side, slot):
        return pltpu.make_async_remote_copy(
            src_ref=cbuf.at[side, slot],
            dst_ref=cbuf.at[side, slot],
            send_sem=f_send.at[slot],
            recv_sem=c_recv.at[side, slot],
            device_id=sibling,
            device_id_type=MESH,
        )

    def r_copy(offset, slot):
        return pltpu.make_async_remote_copy(
            src_ref=pts,
            dst_ref=rbuf.at[slot],
            send_sem=r_send.at[offset],
            recv_sem=r_recv.at[slot],
            device_id=at_hi(partner(hi, offset, nh)),
            device_id_type=MESH,
        )

    def d_copy(offset, slot):
        return pltpu.make_async_remote_copy(
            src_ref=direction,
            dst_ref=dbuf.at[slot],
            send_sem=d_send.at[offset],
            recv_sem=d_recv.at[slot],
            device_id=at_hi(partner(hi, offset, nh)),
            device_id_type=MESH,
        )

    def p_copy(owner, slot):
        return pltpu.make_async_remote_copy(
            src_ref=pout.at[owner],
            dst_ref=pin.at[slot],
            send_sem=p_send.at[owner],
            recv_sem=p_recv.at[slot],
            device_id=at_hi(owner),
            device_id_type=MESH,
        )

    for offset in range(1, nb):
        c_copy(offset, b).start()
    for offset in range(1, nh):
        r_copy(offset, hi).start()
    f_copy(core, b).start()
    sum_r[0].start(own_res_gram)
    for offset in range(1, nh):
        d_copy(offset, hi).start()
    sum_r[1].start(sum_r[0].finish())
    scale = scales[...]
    ones = jnp.ones((8, scale.shape[1]), jnp.float32)
    places = [hi] + [source(hi, offset, nh) for offset in range(1, nh)]
    slots = [b] + [source(b, offset, nb) for offset in range(1, nb)]

    def row_group(first):
        members = range(first, min(first + 2, nh))
        for member in members:
            if member > 0:
                r_copy(member, places[member]).wait_recv()
        raw = [pts[...] if member == 0 else rbuf[places[member]] for member in members]
        left = jnp.concatenate(raw, axis=0) / scale
        return left, 0.5 * nt(ones, left * left)[:1, :]

    def column_set(members):
        blocks = [(side, slots[member]) for member in members for side in (core, 1 - core)]
        right = jnp.concatenate([cbuf[side, slot, :rows] / scale for side, slot in blocks], axis=0)
        right_sq = 0.5 * jnp.sum(right * right, axis=1, keepdims=True)
        return right, right_sq, jnp.concatenate([cbuf[side, slot, rows:] for side, slot in blocks], axis=1)

    def image_part(group, columns):
        left, left_sq = group
        right, right_sq, directions = columns
        return nn(directions, jnp.exp(nt(right, left) - (right_sq + left_sq)))

    def forward(offset):
        c_copy(offset, slots[offset]).wait_recv()
        f_copy(core, slots[offset]).start()

    last = nb - 1
    for offset in range(1, last):
        forward(offset)
    for offset in range(last):
        f_copy(1 - core, slots[offset]).wait_recv()
    group = row_group(0)
    early = column_set(range(last))
    images = image_part(group, early)
    forward(last)
    sum_r[2].start(sum_r[1].finish())
    f_copy(1 - core, slots[last]).wait_recv()
    late = column_set([last])
    images = images + image_part(group, late)
    parts = [images[:, :rows] + noise[0, 0] * direct]
    everything = tuple(jnp.concatenate(pair, axis=axis) for pair, axis in zip(zip(early, late), (0, 0, 1)))
    for first in range(0, nh, 2):
        if first > 0:
            images = image_part(row_group(first), everything)
        for member in range(max(first, 1), min(first + 2, nh)):
            part = images[:, (member - first) * rows : (member - first + 1) * rows]
            pout[places[member]] = part
            p_copy(places[member], hi).start()
            parts.append(part)
    image, others = parts[0], [direct]
    for offset in range(1, nh):
        place = source(hi, offset, nh)
        d_copy(offset, place).wait_recv()
        others.append(dbuf[place])
    own_gram = 0.5 * nt(jnp.concatenate(others + parts, axis=1), jnp.concatenate(parts + others, axis=1))
    sum_a[0].start(pack(own_gram))
    sum_a[1].start(sum_a[0].finish())

    res_gram = unpack(sum_r[2].finish())
    eye = lax.broadcasted_iota(jnp.int32, (rhs, rhs), 0) == lax.broadcasted_iota(jnp.int32, (rhs, rhs), 1)
    res_inverse = eliminate(res_gram, eye.astype(jnp.float32))

    sum_a[2].start(sum_a[1].finish())
    for offset in range(1, nh):
        place = source(hi, offset, nh)
        p_copy(place, place).wait_recv()
        image = image + pin[place]
    sum_bc[0].start(nt(image, jnp.concatenate([res, image], axis=0)))
    sum_bc[1].start(sum_bc[0].finish())
    sum_bc[2].start(sum_bc[1].finish())
    gram = unpack(sum_a[2].finish())
    step = eliminate(gram, res_gram)
    new_res = res - tn(step, image)
    out[0] = iterate[...] + tn(step, direct)
    out[1] = new_res
    both = sum_bc[2].finish()
    cross, square = both[:, :rhs], both[:, rhs:]
    moved = nn(square, step) - cross
    new_gram = res_gram + tn(
        jnp.concatenate([step, -cross], axis=0), jnp.concatenate([moved, step], axis=0)
    )
    correction = nn(res_inverse, new_gram)
    out[2] = new_res + tn(correction, direct)

    for offset in range(1, nb):
        c_copy(offset, b).wait_send()
    for slot in range(nb):
        f_copy(core, slot).wait_send()
    for offset in range(1, nh):
        r_copy(offset, hi).wait_send()
        d_copy(offset, hi).wait_send()
        p_copy(source(hi, offset, nh), hi).wait_send()


def split(stacked, out_i, out_r, out_d):
    for place, out in enumerate((out_i, out_r, out_d)):
        out[...] = stacked[place]


def solution(mesh):
    nb, ni = mesh.shape["blk"], mesh.shape["inner"]
    nh = ni // 2

    def on_device(points, lengthscales, noise_level, iterate, residual, direction):
        rows, features = points.shape
        rhs = direction.shape[1]
        f32, dma = jnp.float32, pltpu.SemaphoreType.DMA
        scratch = [
            pltpu.VMEM((2, nb, rows + rhs, features), f32),
            dma((nb,)),
            dma((2, nb)),
            dma((nb,)),
            pltpu.VMEM((nh, rows, features), f32),
            dma((nh,)),
            dma((nh,)),
            pltpu.VMEM((nh, rhs, rows), f32),
            dma((nh,)),
            dma((nh,)),
            pltpu.VMEM((nh, rhs, rows), f32),
            pltpu.VMEM((nh, rhs, rows), f32),
            dma((nh,)),
            dma((nh,)),
        ]
        for height in (rhs // 2, rhs // 2, rhs):
            for n in (2, nb, nh):
                scratch += [
                    pltpu.VMEM((height, 2 * rhs), f32),
                    pltpu.VMEM((n, height, 2 * rhs), f32),
                    dma((n,)),
                    dma((n,)),
                ]
        vmem = pl.BlockSpec(memory_space=pltpu.VMEM)
        out = jax.ShapeDtypeStruct((rhs, rows), f32)
        stacked = pl.pallas_call(
            functools.partial(body, (nb, nh, rows, rhs)),
            out_shape=jax.ShapeDtypeStruct((3, rhs, rows), f32),
            in_specs=[vmem, vmem, pl.BlockSpec(memory_space=pltpu.SMEM), vmem, vmem, vmem],
            out_specs=vmem,
            scratch_shapes=scratch,
            compiler_params=pltpu.CompilerParams(collective_id=0, has_side_effects=True),
            name="cg_step",
        )(points, lengthscales[None, :], noise_level[None, :], iterate.T, residual.T, direction.T)
        results = pl.pallas_call(
            split, out_shape=(out, out, out), in_specs=[vmem], out_specs=(vmem, vmem, vmem), name="split"
        )(stacked)
        return tuple(result.T for result in results)

    rows_spec = P(("blk", "inner"), None)
    return jax.shard_map(
        on_device,
        mesh=mesh,
        in_specs=(rows_spec, P(), P(), rows_spec, rows_spec, rows_spec),
        out_specs=(rows_spec, rows_spec, rows_spec),
        check_vma=False,
    )
```

```python
import functools

import jax
import jax.numpy as jnp
from jax import lax
from jax.experimental import pallas as pl
from jax.experimental.pallas import tpu as pltpu
from jax.sharding import PartitionSpec as P

MESH = pl.DeviceIdType.MESH
HI = lax.Precision.HIGHEST


def mm(left, right, dims):
    return lax.dot_general(left, right, (dims, ((), ())), precision=HI, preferred_element_type=jnp.float32)


def nn(left, right):
    return mm(left, right, ((1,), (0,)))


def nt(left, right):
    return mm(left, right, ((1,), (1,)))


def tn(left, right):
    return mm(left, right, ((0,), (0,)))


def pack(value):
    half = value.shape[0] // 2
    return jnp.concatenate([value[:half], value[half:]], axis=1)


def unpack(value):
    half = value.shape[1] // 2
    return jnp.concatenate([value[:, :half], value[:, half:]], axis=0)


def partner(me, offset, n):
    if n & (n - 1):
        return lax.rem(me + offset, n)
    place, bit = me, 1
    while bit < n:
        if offset & bit:
            place = place + bit - 2 * bit * lax.rem(me // bit, 2)
        bit *= 2
    return place


def source(me, offset, n):
    if n & (n - 1):
        return lax.rem(me + n - offset, n)
    return partner(me, offset, n)


def eliminate(matrix, rhs_side):
    n = matrix.shape[0]
    work = jnp.concatenate([matrix, rhs_side], axis=1)
    rows = lax.broadcasted_iota(jnp.int32, work.shape, 0)
    for k in range(0, n, 2):
        column0 = jnp.broadcast_to(work[:, k : k + 1], work.shape)
        column1 = jnp.broadcast_to(work[:, k + 1 : k + 2], work.shape)
        row0, row1 = work[k : k + 1], work[k + 1 : k + 2]
        upper = column1[k : k + 1]
        inverse = 1.0 / column0[k : k + 1]
        lower = column0[k + 1 : k + 2] * inverse
        second = (row1 - lower * row0) / (column1[k + 1 : k + 2] - lower * upper)
        first = (row0 - upper * second) * inverse
        below = work - column0 * first - column1 * second
        work = jnp.where(rows == k, first, jnp.where(rows == k + 1, second, below))
    return work[:, n:]


class Exchange:
    def __init__(self, src, slots, send, recv, me, n, device):
        self.src, self.slots, self.send, self.recv = src, slots, send, recv
        self.me, self.n, self.device = me, n, device

    def copy(self, offset, slot):
        return pltpu.make_async_remote_copy(
            src_ref=self.src,
            dst_ref=self.slots.at[slot],
            send_sem=self.send.at[offset],
            recv_sem=self.recv.at[slot],
            device_id=self.device(partner(self.me, offset, self.n)),
            device_id_type=MESH,
        )

    def start(self, value):
        self.src[...] = value
        for offset in range(1, self.n):
            self.copy(offset, self.me).start()

    def finish(self):
        total = self.src[...]
        for offset in range(1, self.n):
            slot = source(self.me, offset, self.n)
            self.copy(offset, slot).wait_recv()
            total = total + self.slots[slot]
        for offset in range(1, self.n):
            self.copy(offset, self.me).wait_send()
        return total


def body(sizes, pts, scales, noise, iterate, residual, direction, out, *scratch):
    nb, nh, rows, rhs = sizes
    cbuf, c_send, c_recv, f_send, rbuf, r_send, r_recv = scratch[:7]
    dbuf, d_send, d_recv, pout, pin, p_send, p_recv = scratch[7:14]
    rest = scratch[14:]
    b = lax.axis_index("blk")
    i = lax.axis_index("inner")
    core = lax.rem(i, 2)
    hi = i // 2
    sibling = {"inner": hi * 2 + 1 - core}

    def at_blk(place):
        return {"blk": place}

    def at_hi(place):
        return {"inner": place * 2 + core}

    def at_core(place):
        return {"inner": hi * 2 + place}

    ways = ((core, 2, at_core), (b, nb, at_blk), (hi, nh, at_hi))
    sums = []
    for which in range(3):
        stages = []
        for stage, (me, n, device) in enumerate(ways):
            src, slots, send, recv = rest[(which * 3 + stage) * 4 : (which * 3 + stage) * 4 + 4]
            stages.append(Exchange(src, slots, send, recv, me, n, device))
        sums.append(stages)
    sum_r, sum_a, sum_bc = sums

    barrier = pltpu.get_barrier_semaphore()
    for offset in range(1, nb):
        pl.semaphore_signal(barrier, inc=1, device_id=at_blk(partner(b, offset, nb)), device_id_type=MESH)
    for offset in range(1, nh):
        pl.semaphore_signal(barrier, inc=1, device_id=at_hi(partner(hi, offset, nh)), device_id_type=MESH)
    pl.semaphore_signal(barrier, inc=1, device_id=sibling, device_id_type=MESH)
    cbuf[core, b, :rows] = pts[...]
    cbuf[core, b, rows:] = direction[...]
    res = residual[...]
    direct = direction[...]
    own_res_gram = pack(nt(res, res))
    pl.semaphore_wait(barrier, nb + nh - 1)

    def c_copy(offset, slot):
        return pltpu.make_async_remote_copy(
            src_ref=cbuf.at[core, slot],
            dst_ref=cbuf.at[core, slot],
            send_sem=c_send.at[offset],
            recv_sem=c_recv.at[core, slot],
            device_id=at_blk(partner(b, offset, nb)),
            device_id_type=MESH,
        )

    def f_copy(side, slot):
        return pltpu.make_async_remote_copy(
            src_ref=cbuf.at[side, slot],
            dst_ref=cbuf.at[side, slot],
            send_sem=f_send.at[slot],
            recv_sem=c_recv.at[side, slot],
            device_id=sibling,
            device_id_type=MESH,
        )

    def r_copy(offset, slot):
        return pltpu.make_async_remote_copy(
            src_ref=pts,
            dst_ref=rbuf.at[slot],
            send_sem=r_send.at[offset],
            recv_sem=r_recv.at[slot],
            device_id=at_hi(partner(hi, offset, nh)),
            device_id_type=MESH,
        )

    def d_copy(offset, slot):
        return pltpu.make_async_remote_copy(
            src_ref=direction,
            dst_ref=dbuf.at[slot],
            send_sem=d_send.at[offset],
            recv_sem=d_recv.at[slot],
            device_id=at_hi(partner(hi, offset, nh)),
            device_id_type=MESH,
        )

    def p_copy(owner, slot):
        return pltpu.make_async_remote_copy(
            src_ref=pout.at[owner],
            dst_ref=pin.at[slot],
            send_sem=p_send.at[owner],
            recv_sem=p_recv.at[slot],
            device_id=at_hi(owner),
            device_id_type=MESH,
        )

    for offset in range(1, nb):
        c_copy(offset, b).start()
    for offset in range(1, nh):
        r_copy(offset, hi).start()
    f_copy(core, b).start()
    sum_r[0].start(own_res_gram)
    for offset in range(1, nh):
        d_copy(offset, hi).start()
    sum_r[1].start(sum_r[0].finish())
    scale = scales[...]
    ones = jnp.ones((8, scale.shape[1]), jnp.float32)
    places = [hi] + [source(hi, offset, nh) for offset in range(1, nh)]
    slots = [b] + [source(b, offset, nb) for offset in range(1, nb)]

    def row_group(first):
        members = range(first, min(first + 2, nh))
        for member in members:
            if member > 0:
                r_copy(member, places[member]).wait_recv()
        raw = [pts[...] if member == 0 else rbuf[places[member]] for member in members]
        left = jnp.concatenate(raw, axis=0) / scale
        return left, 0.5 * nt(ones, left * left)[:1, :]

    def column_set(members):
        blocks = [(side, slots[member]) for member in members for side in (core, 1 - core)]
        right = jnp.concatenate([cbuf[side, slot, :rows] / scale for side, slot in blocks], axis=0)
        right_sq = 0.5 * jnp.sum(right * right, axis=1, keepdims=True)
        return right, right_sq, jnp.concatenate([cbuf[side, slot, rows:] for side, slot in blocks], axis=1)

    def image_part(group, columns):
        left, left_sq = group
        right, right_sq, directions = columns
        return nn(directions, jnp.exp(nt(right, left) - (right_sq + left_sq)))

    def forward(offset):
        c_copy(offset, slots[offset]).wait_recv()
        f_copy(core, slots[offset]).start()

    last = nb - 1
    for offset in range(1, last):
        forward(offset)
    for offset in range(last):
        f_copy(1 - core, slots[offset]).wait_recv()
    group = row_group(0)
    early = column_set(range(last))
    images = image_part(group, early)
    forward(last)
    sum_r[2].start(sum_r[1].finish())
    f_copy(1 - core, slots[last]).wait_recv()
    late = column_set([last])
    images = images + image_part(group, late)
    parts = [images[:, :rows] + noise[0, 0] * direct]
    everything = tuple(jnp.concatenate(pair, axis=axis) for pair, axis in zip(zip(early, late), (0, 0, 1)))
    for first in range(0, nh, 2):
        if first > 0:
            images = image_part(row_group(first), everything)
        for member in range(max(first, 1), min(first + 2, nh)):
            part = images[:, (member - first) * rows : (member - first + 1) * rows]
            pout[places[member]] = part
            p_copy(places[member], hi).start()
            parts.append(part)
    image, others = parts[0], [direct]
    for offset in range(1, nh):
        place = source(hi, offset, nh)
        d_copy(offset, place).wait_recv()
        others.append(dbuf[place])
    own_gram = 0.5 * nt(jnp.concatenate(others + parts, axis=1), jnp.concatenate(parts + others, axis=1))
    sum_a[0].start(pack(own_gram))
    sum_a[1].start(sum_a[0].finish())

    for offset in range(1, nh):
        place = source(hi, offset, nh)
        p_copy(place, place).wait_recv()
        image = image + pin[place]
    sum_bc[0].start(nt(image, jnp.concatenate([res, image], axis=0)))
    sum_a[2].start(sum_a[1].finish())
    sum_bc[1].start(sum_bc[0].finish())
    res_gram = unpack(sum_r[2].finish())
    unit = lax.broadcasted_iota(jnp.int32, (rhs, rhs), 0) == lax.broadcasted_iota(jnp.int32, (rhs, rhs), 1)
    unit = unit.astype(jnp.float32)
    res_inverse = eliminate(res_gram, unit)
    sum_bc[2].start(sum_bc[1].finish())
    gram = unpack(sum_a[2].finish())
    step = eliminate(gram, res_gram)
    new_res = res - tn(step, image)
    out[0] = iterate[...] + tn(step, direct)
    out[1] = new_res
    ahead = nt(res_inverse, step)
    both = sum_bc[2].finish()
    cross, square = both[:, :rhs], both[:, rhs:]
    turned = nt(res_inverse, cross)
    correction = unit - nn(ahead, cross) + nn(
        jnp.concatenate([ahead, -turned], axis=1), jnp.concatenate([nn(square, step), step], axis=0)
    )
    out[2] = new_res + tn(correction, direct)

    for offset in range(1, nb):
        c_copy(offset, b).wait_send()
    for slot in range(nb):
        f_copy(core, slot).wait_send()
    for offset in range(1, nh):
        r_copy(offset, hi).wait_send()
        d_copy(offset, hi).wait_send()
        p_copy(source(hi, offset, nh), hi).wait_send()


def split(stacked, out_i, out_r, out_d):
    for place, out in enumerate((out_i, out_r, out_d)):
        out[...] = stacked[place]


def solution(mesh):
    nb, ni = mesh.shape["blk"], mesh.shape["inner"]
    nh = ni // 2

    def on_device(points, lengthscales, noise_level, iterate, residual, direction):
        rows, features = points.shape
        rhs = direction.shape[1]
        f32, dma = jnp.float32, pltpu.SemaphoreType.DMA
        scratch = [
            pltpu.VMEM((2, nb, rows + rhs, features), f32),
            dma((nb,)),
            dma((2, nb)),
            dma((nb,)),
            pltpu.VMEM((nh, rows, features), f32),
            dma((nh,)),
            dma((nh,)),
            pltpu.VMEM((nh, rhs, rows), f32),
            dma((nh,)),
            dma((nh,)),
            pltpu.VMEM((nh, rhs, rows), f32),
            pltpu.VMEM((nh, rhs, rows), f32),
            dma((nh,)),
            dma((nh,)),
        ]
        for height in (rhs // 2, rhs // 2, rhs):
            for n in (2, nb, nh):
                scratch += [
                    pltpu.VMEM((height, 2 * rhs), f32),
                    pltpu.VMEM((n, height, 2 * rhs), f32),
                    dma((n,)),
                    dma((n,)),
                ]
        vmem = pl.BlockSpec(memory_space=pltpu.VMEM)
        out = jax.ShapeDtypeStruct((rhs, rows), f32)
        stacked = pl.pallas_call(
            functools.partial(body, (nb, nh, rows, rhs)),
            out_shape=jax.ShapeDtypeStruct((3, rhs, rows), f32),
            in_specs=[vmem, vmem, pl.BlockSpec(memory_space=pltpu.SMEM), vmem, vmem, vmem],
            out_specs=vmem,
            scratch_shapes=scratch,
            compiler_params=pltpu.CompilerParams(collective_id=0, has_side_effects=True),
            name="cg_step",
        )(points, lengthscales[None, :], noise_level[None, :], iterate.T, residual.T, direction.T)
        results = pl.pallas_call(
            split, out_shape=(out, out, out), in_specs=[vmem], out_specs=(vmem, vmem, vmem), name="split"
        )(stacked)
        return tuple(result.T for result in results)

    rows_spec = P(("blk", "inner"), None)
    return jax.shard_map(
        on_device,
        mesh=mesh,
        in_specs=(rows_spec, P(), P(), rows_spec, rows_spec, rows_spec),
        out_specs=(rows_spec, rows_spec, rows_spec),
        check_vma=False,
    )
```
